256 devices in a mesh: ka: 4 (over z_hi, core), fit: 64 (over x, y, z_lo).
Axes of the slice: x: 4, y: 4, z: 8 (z_hi: 2, z_lo: 4; z = z_hi * 4 + z_lo), core: 2. Of those that a mesh axis runs over, the one named last changes fastest.
Arguments:
- integrals: bfloat16 [3, 4, 64, 48, 64, 128], P(None, 'ka', 'fit'), may hold values from -0.3125 to 0.3125
- block_lists: int32 [3, 4, 64, 2, 48], P(None, 'ka', 'fit'), may hold values from 0 to 15, as said below
- coeff: bfloat16 [4, 2, 1024, 256], P('ka', None, 'fit'), may hold values from -6 to 6
- match: int32 [3, 4], replicated, may hold values from 0 to 3, each once within a row
- ex_blocks: int32 [4, 2, 64], P('ka'), may hold values from 0 to 15, as said below
Outputs:
- exchange: float32 [4, 4096, 128], P('ka', 'fit')
The draws below stay inside these ranges and needn't reach their ends.
Inputs may be any that keep to these rules, and one draw needn't show every extreme that they name: `block_lists`: each integral matrix lists 48 distinct blocks; each entry is a block index below 16, row first then column. `ex_blocks`: each k-point lists 64 distinct blocks, none on the diagonal (row block differs from column block).
All inputs are finite; a program needn't handle non-finite values.
Results may differ from the reference program's by a relative error of at most 0.0036.
Values may be sent and summed in bfloat16 or wider, within the bound.
A program may use at most 128 MiB of HBM per device.

```python
import jax
import jax.numpy as jnp
from jax import lax

NAO = 1024
NOCC = 256
EDGE = 64
NQ = 3
NBLK = 48
EXB = 64
NK = 4
NAUX = 64
NB = 16


def draw_block_lists(key, part):
    keys = jax.random.split(jax.random.fold_in(key, 11), NQ * NK * NAUX)
    ids = jax.vmap(lambda one: jax.random.permutation(one, NB * NB)[:NBLK])(keys)
    lists = jnp.stack([ids // NB, ids % NB], axis=1)
    return lists.reshape(NQ, NK, NAUX, 2, NBLK).astype(jnp.int32)


def draw_ex_blocks(key, part):
    keys = jax.random.split(jax.random.fold_in(key, 23), NK)
    ids = jax.vmap(lambda one: jax.random.permutation(one, NB * (NB - 1))[:EXB])(keys)
    rowblk = ids // (NB - 1)
    other = ids % (NB - 1)
    colblk = other + (other >= rowblk).astype(jnp.int32)
    return jnp.stack([rowblk, colblk], axis=1).astype(jnp.int32)


def level_of(stream_key, extent, cuts, least, high):
    def one(dim, shards_of):
        steps = jax.random.uniform(jax.random.fold_in(jax.random.fold_in(stream_key, 6), dim), (shards_of,), jnp.float32, least / len(cuts), high / len(cuts))
        return jnp.repeat(jnp.exp(steps), extent[dim] // shards_of).reshape((-1,) + (1,) * (len(extent) - dim - 1))

    gain = one(*cuts[0])
    for cut in cuts[1:]:
        gain = gain * one(*cut)
    return gain


def gaussian(rng, extent, scale, bound, cuts=(), kind=jnp.bfloat16):
    array = scale * jax.random.normal(rng, extent, jnp.float32)
    if cuts:
        array = array * level_of(rng, extent, cuts, -0.22, 0.18)
    return jnp.clip(array, -bound, bound).astype(kind)


def setup_inputs(seed: int = 0) -> dict:
    key_list = jax.random.split(jax.random.key(seed), 6)
    return {
        "integrals": gaussian(key_list[0], (NQ, NK, NAUX, NBLK, EDGE, 2 * EDGE), (8 * NBLK) ** -0.5, 0.3125, ((1, 4), (2, 64))),
        "block_lists": draw_block_lists(jax.random.fold_in(key_list[5], 71), 0),
        "coeff": gaussian(key_list[2], (NK, 2, NAO, NOCC), 1.0, 6.0, ((0, 4), (2, 64))),
        "match": jax.vmap(lambda own: jax.random.permutation(own, NK))(jax.random.split(key_list[3], NQ)).reshape((NQ, NK)).astype(jnp.int32),
        "ex_blocks": draw_ex_blocks(jax.random.fold_in(key_list[5], 71), 0),
    }


def block_operands(coeff_one, edge):
    nblocks = coeff_one.shape[1] // edge
    real = coeff_one[0].reshape(nblocks, edge, -1)
    imag = coeff_one[1].reshape(nblocks, edge, -1)
    upper = jnp.concatenate([real, imag], axis=2)
    lower = jnp.concatenate([-imag, real], axis=2)
    return jnp.concatenate([upper, lower], axis=1)


def half_transform(lmat, lists, operands):
    nblocks = operands.shape[0]
    picked = jnp.take(operands, lists[1], axis=0).astype(jnp.float32)
    prods = jnp.einsum("bmi,bij->bmj", lmat.astype(jnp.float32), picked, precision=lax.Precision.HIGHEST)
    onehot = (lists[0][None, :] == jnp.arange(nblocks, dtype=jnp.int32)[:, None]).astype(jnp.float32)
    rows = jnp.einsum("rb,bmj->rmj", onehot, prods, precision=lax.Precision.HIGHEST)
    return rows.astype(jnp.bfloat16)


def exchange_blocks(xmat, listed):
    occ = xmat.shape[2] // 2
    left = jnp.take(xmat, listed[0], axis=0).astype(jnp.float32)
    right = jnp.take(xmat, listed[1], axis=0).astype(jnp.float32)
    swapped = jnp.concatenate([left[:, :, occ:], -left[:, :, :occ]], axis=2)
    kreal = jnp.einsum("emj,enj->emn", left, right, precision=lax.Precision.HIGHEST)
    kimag = jnp.einsum("emj,enj->emn", swapped, right, precision=lax.Precision.HIGHEST)
    return jnp.concatenate([kreal, kimag], axis=2)


def reference(integrals, block_lists, coeff, match, ex_blocks):
    edge = integrals.shape[4]
    operands_all = jnp.stack([block_operands(coeff[k], edge) for k in range(NK)])
    factor = -((NQ * NAUX * NOCC) ** -0.5)
    outs = []
    for kpt in range(NK):
        def step(index, acc):
            qq = index // NAUX
            pp = index % NAUX
            partner = match[qq, kpt]
            operands = operands_all[partner]
            xmat = half_transform(integrals[qq, kpt, pp], block_lists[qq, kpt, pp], operands)
            xmat = lax.optimization_barrier(xmat)
            return acc + exchange_blocks(xmat, ex_blocks[kpt])
        start = jnp.zeros((EXB, edge, 2 * edge), jnp.float32)
        acc = lax.fori_loop(0, NQ * NAUX, step, start)
        outs.append((acc * factor).reshape(EXB * edge, 2 * edge))
    return jnp.stack(outs)
```

```python
import jax
import jax.numpy as jnp
from jax import lax
from jax.experimental import pallas as pl
from jax.experimental.pallas import tpu as pltpu
from jax.sharding import PartitionSpec as P

MESH = pl.DeviceIdType.MESH
NT = (((1,), (1,)), ((), ()))
F32 = jnp.float32
BF16 = jnp.bfloat16


def place():
    ka, fit = lax.axis_index("ka"), lax.axis_index("fit")
    x, y, zl = fit // 16, (fit // 4) % 4, fit % 4
    return ka // 2, ka % 2, x, y, zl


def device(zh, c, x, y, zl):
    return (zh * 2 + c, x * 16 + y * 4 + zl)


def rcopy(src, dst, ssem, rsem, dev):
    return pltpu.make_async_remote_copy(
        src_ref=src, dst_ref=dst, send_sem=ssem, recv_sem=rsem, device_id=dev, device_id_type=MESH
    )


def greet(devices):
    barrier = pltpu.get_barrier_semaphore()
    for dev in devices:
        pl.semaphore_signal(barrier, inc=1, device_id=dev, device_id_type=MESH)
    pl.semaphore_wait(barrier, len(devices))


def gather_kernel(coeff, out, g, lsem, zs, zr, rs, rr, bs, br):
    zh, c, x, y, zl = place()
    z = zh * 4 + zl
    own = pl.ds(pl.multiple_of(zl * 16, 16), 16)
    loads = []
    for h in range(2):
        for s in range(2):
            cp = pltpu.make_async_copy(
                coeff.at[0, s, :, h * 128 : (h + 1) * 128], g.at[zh, c, h, s, x, y, own], lsem.at[h * 2 + s]
            )
            cp.start()
            loads.append(cp)

    def nb(dx, dy):
        return device(zh, c, (x + dx + 4) % 4, (y + dy + 4) % 4, zl)

    zdev = []
    for j in range(1, 8):
        zz = (z + j) % 8
        zdev.append(device(zz // 4, c, x, y, zz % 4))
    sib = device(zh, 1 - c, x, y, zl)
    greet(zdev + [nb(1, 0), nb(-1, 0), nb(0, 1), nb(0, -1), sib])
    for cp in loads:
        cp.wait()

    piece = g.at[zh, c, :, :, x, y, own]
    zc = [rcopy(piece, piece, zs.at[j], zr.at[j], zdev[j]) for j in range(7)]
    for cp in zc:
        cp.start()
    for cp in zc:
        cp.wait()

    started = []

    def ring(n, part, up, down, block):
        first = {}
        for i, dev in ((0, up), (1, down)):
            for s in range(2):
                cp = rcopy(block(0, s), block(0, s), rs.at[n, i, s], rr.at[n, i, s], dev)
                cp.start()
                first[i, s] = cp
        return first

    def relay(n, first, up, down, block):
        first[0, 0].wait_recv()
        a = rcopy(block(-1, 0), block(-1, 0), rs.at[n, 2, 0], rr.at[n, 2, 0], up)
        a.start()
        first[1, 1].wait_recv()
        b = rcopy(block(1, 1), block(1, 1), rs.at[n, 2, 1], rr.at[n, 2, 1], down)
        b.start()
        first[0, 1].wait_recv()
        first[1, 0].wait_recv()
        return [a, b]

    def blk_a2(d, s):
        return g.at[:, c, 0, s, x, (y + d + 4) % 4]

    def blk_b2(d, s):
        return g.at[:, c, 1, s, (x + d + 4) % 4, y]

    def blk_a3(d, s):
        return g.at[:, c, 0, s, (x + d + 4) % 4]

    def blk_b3(d, s):
        return g.at[:, c, 1, s, :, (y + d + 4) % 4]

    ax = (nb(1, 0), nb(-1, 0))
    ay = (nb(0, 1), nb(0, -1))
    fa = ring(0, 0, *ay, blk_a2)
    fb = ring(1, 1, *ax, blk_b2)
    ra = relay(0, fa, *ay, blk_a2)
    rb = relay(1, fb, *ax, blk_b2)
    for cp in ra + rb:
        cp.wait_recv()
    fa3 = ring(2, 0, *ax, blk_a3)
    fb3 = ring(3, 1, *ay, blk_b3)
    sibs = []

    def to_sib(i, block, d):
        for s in range(2):
            cp = rcopy(block(d, s), block(d, s), bs.at[i, s], br.at[i, s], sib)
            cp.start()
            sibs.append(cp)

    to_sib(0, blk_a3, 0)
    to_sib(1, blk_b3, 0)
    ra3 = relay(2, fa3, *ax, blk_a3)
    rb3 = relay(3, fb3, *ay, blk_b3)
    to_sib(2, blk_a3, 1)
    to_sib(3, blk_b3, 1)
    to_sib(4, blk_a3, -1)
    to_sib(5, blk_b3, -1)
    for cp in ra3 + rb3:
        cp.wait_recv()
    to_sib(6, blk_a3, 2)
    to_sib(7, blk_b3, 2)
    for cp in sibs:
        cp.wait()
    for f in (fa, fb, fa3, fb3):
        for cp in f.values():
            cp.wait_send()
    for cp in ra + rb + ra3 + rb3:
        cp.wait_send()
    cp = pltpu.make_async_copy(g, out, lsem.at[0])
    cp.start()
    cp.wait()


def gather(coeff):
    shape = (2, 2, 2, 2, 4, 4, 64, 128)
    dma = pltpu.SemaphoreType.DMA
    return pl.pallas_call(
        gather_kernel,
        out_shape=jax.ShapeDtypeStruct(shape, BF16),
        in_specs=[pl.BlockSpec(memory_space=pl.ANY)],
        out_specs=pl.BlockSpec(memory_space=pl.ANY),
        scratch_shapes=[
            pltpu.VMEM(shape, BF16),
            dma((4,)),
            dma((7,)),
            dma((7,)),
            dma((4, 3, 2)),
            dma((4, 3, 2)),
            dma((8, 2)),
            dma((8, 2)),
        ],
        compiler_params=pltpu.CompilerParams(collective_id=0, has_side_effects=True),
        name="gather",
    )(coeff)


def local_kernel(idx, part, ex, lin, g, sf, sb, lv, ld, xs):
    lv[0:144] = lin[...]
    lv[144] = jnp.zeros((64, 128), BF16)

    @pl.loop(0, 48)
    def _(i):
        q, c = i // 16, i % 16
        for r in range(16):
            ld[q, c, r * 64 : (r + 1) * 64, :] = lv[idx[q, r * 16 + c]]

    @pl.loop(0, 24)
    def _(i):
        q, h, t = i // 8, (i // 4) % 2, i % 4
        pk = part[q]
        acc = jnp.zeros((256, 256), F32)
        rows = pl.ds(pl.multiple_of(t * 256, 256), 256)
        for cp in range(8):
            lhs = jnp.concatenate([ld[q, 2 * cp, rows, :], ld[q, 2 * cp + 1, rows, :]], axis=1)
            parts = []
            for c in (2 * cp, 2 * cp + 1):
                re = g[pk, h, 0, c * 64 : (c + 1) * 64, :]
                im = g[pk, h, 1, c * 64 : (c + 1) * 64, :]
                parts += [jnp.concatenate([re, im], axis=1), jnp.concatenate([-im, re], axis=1)]
            acc += jnp.dot(lhs, jnp.concatenate(parts, axis=0), preferred_element_type=F32)
        xs[q, h, rows, :] = acc.astype(BF16)

    @pl.loop(0, 16)
    def _(i):
        for u in range(4):
            e = i * 4 + u
            rr = pl.ds(pl.multiple_of(ex[0, e] * 64, 64), 64)
            ss = pl.ds(pl.multiple_of(ex[1, e] * 64, 64), 64)
            acc = jnp.zeros((64, 128), F32)
            for q in range(3):
                for h in range(2):
                    a, b = xs[q, h, rr, :], xs[q, h, ss, :]
                    w = jnp.concatenate([-b[:, 128:], b[:, :128]], axis=1)
                    acc += lax.dot_general(a, jnp.concatenate([b, w], axis=0), NT, preferred_element_type=F32)
            for p in range(2):
                piece = acc[p * 32 : (p + 1) * 32]
                sf[p, i // 4, i % 4, u] = piece
                sb[p, i // 4, i % 4, u] = piece.astype(BF16)


def local(idx, part, ex, lin, g):
    smem = pl.BlockSpec(memory_space=pltpu.SMEM)
    vmem = pl.BlockSpec(memory_space=pltpu.VMEM)
    shape = (2, 4, 4, 4, 32, 128)
    return pl.pallas_call(
        local_kernel,
        out_shape=(jax.ShapeDtypeStruct(shape, F32), jax.ShapeDtypeStruct(shape, BF16)),
        in_specs=[smem] * 3 + [vmem] * 2,
        out_specs=(vmem, vmem),
        scratch_shapes=[
            pltpu.VMEM((145, 64, 128), BF16),
            pltpu.VMEM((3, 16, 1024, 128), BF16),
            pltpu.VMEM((3, 2, 1024, 256), BF16),
        ],
        compiler_params=pltpu.CompilerParams(vmem_limit_bytes=56 * 2**20),
        name="local",
    )(idx, part, ex, lin, g)


def scatter_kernel(factor, sf, sb, out, ra, rb, t, a1f, a1b, qa, qb, qt, a2f, a2b, zin, ss, rs, zs, zr):
    zh, c, x, y, zl = place()

    def nb(dx, dy):
        return device(zh, c, (x + dx + 4) % 4, (y + dy + 4) % 4, zl)

    zdev = [device(zh, c, x, y, (zl + j) % 4) for j in range(1, 4)]
    ax = (nb(1, 0), nb(-1, 0))
    ay = (nb(0, 1), nb(0, -1))
    greet(zdev + list(ax) + list(ay))

    def begin(n, axis, blk, r1, r2):
        up, down = axis
        out = []
        out.append(rcopy(blk(2, 0), r1.at[0], ss.at[n, 0], rs.at[n, 0], up))
        out.append(rcopy(blk(2, 1), r1.at[1], ss.at[n, 1], rs.at[n, 1], down))
        out.append(rcopy(blk(1, 1), r2.at[0], ss.at[n, 2], rs.at[n, 2], up))
        out.append(rcopy(blk(-1, 0), r2.at[1], ss.at[n, 3], rs.at[n, 3], down))
        for cp in out:
            cp.start()
        return out

    def middle(n, axis, first, val, r1, tmp, r3):
        out = []
        for i in range(2):
            first[i].wait_recv()
            tmp[i] = (r1[i].astype(F32) + val((1, -1)[i], i)).astype(BF16)
            cp = rcopy(tmp.at[i], r3.at[i], ss.at[n, 4 + i], rs.at[n, 4 + i], axis[i])
            cp.start()
            out.append(cp)
        return out

    def blk1(p):
        def f(d, i):
            j = (((x if p == 0 else y) + d + 4) % 4)
            if p == 0:
                return sb.at[0, j, 2 * i : 2 * i + 2]
            return sb.at[1, 2 * i : 2 * i + 2, j]

        return f

    def val1(p):
        def f(d, i):
            j = (((x if p == 0 else y) + d + 4) % 4)
            if p == 0:
                return sf[0, j, 2 * i : 2 * i + 2]
            return sf[1, 2 * i : 2 * i + 2, j]

        return f

    axis1, axis2 = (ax, ay), (ay, ax)
    first = [begin(p, axis1[p], blk1(p), ra.at[p, 0], ra.at[p, 1]) for p in range(2)]
    mid = [middle(p, axis1[p], first[p], val1(p), ra.at[p, 0], t.at[p], rb.at[p]) for p in range(2)]
    first2 = []
    sent = first + mid

    def blk2(p):
        return lambda d, i: a1b.at[p, ((y if p == 0 else x) + d + 4) % 4, 2 * i : 2 * i + 2]

    def val2(p):
        return lambda d, i: a1f[p, ((y if p == 0 else x) + d + 4) % 4, 2 * i : 2 * i + 2]

    for p in range(2):
        first[p][2].wait_recv()
        first[p][3].wait_recv()
        for i in range(2):
            mid[p][i].wait_recv()
            v = val1(p)(0, i) + ra[p, 1, 1 - i].astype(F32) + rb[p, i].astype(F32)
            a1f[p, 2 * i : 2 * i + 2] = v
            a1b[p, 2 * i : 2 * i + 2] = v.astype(BF16)
        first2.append(begin(2 + p, axis2[p], blk2(p), qa.at[p, 0], qa.at[p, 1]))
    mid2 = [middle(2 + p, axis2[p], first2[p], val2(p), qa.at[p, 0], qt.at[p], qb.at[p]) for p in range(2)]
    for p in range(2):
        first2[p][2].wait_recv()
        first2[p][3].wait_recv()
        for i in range(2):
            mid2[p][i].wait_recv()
            v = val2(p)(0, i) + qa[p, 1, 1 - i].astype(F32) + qb[p, i].astype(F32)
            a2f[p, 2 * i : 2 * i + 2] = v
            a2b[p, 2 * i : 2 * i + 2] = v.astype(BF16)
    zc = []
    for j in range(3):
        cp = rcopy(a2b.at[:, (zl + j + 1) % 4], zin.at[j], zs.at[j], zr.at[j], zdev[j])
        cp.start()
        zc.append(cp)
    total = a2f[:, zl]
    for j in range(3):
        zc[j].wait_recv()
        total = total + zin[j].astype(F32)
    total = total * factor
    out[0:32] = total[0]
    out[32:64] = total[1]
    for cp in zc:
        cp.wait_send()
    for cps in sent + first2 + mid2:
        for cp in cps:
            cp.wait_send()


def scatter(factor, sf, sb):
    vmem = pl.BlockSpec(memory_space=pltpu.VMEM)
    dma = pltpu.SemaphoreType.DMA
    half, quarter = (2, 4, 32, 128), (2, 32, 128)

    def kern(*refs):
        scatter_kernel(factor, *refs)

    return pl.pallas_call(
        kern,
        out_shape=jax.ShapeDtypeStruct((64, 128), F32),
        in_specs=[vmem, vmem],
        out_specs=vmem,
        scratch_shapes=[
            pltpu.VMEM((2, 2, 2) + half, BF16),
            pltpu.VMEM((2, 2) + half, BF16),
            pltpu.VMEM((2, 2) + half, BF16),
            pltpu.VMEM((2, 4, 4, 32, 128), F32),
            pltpu.VMEM((2, 4, 4, 32, 128), BF16),
            pltpu.VMEM((2, 2, 2) + quarter, BF16),
            pltpu.VMEM((2, 2) + quarter, BF16),
            pltpu.VMEM((2, 2) + quarter, BF16),
            pltpu.VMEM((2, 4, 32, 128), F32),
            pltpu.VMEM((2, 4, 32, 128), BF16),
            pltpu.VMEM((3, 2, 32, 128), BF16),
            dma((4, 6)),
            dma((4, 6)),
            dma((3,)),
            dma((3,)),
        ],
        compiler_params=pltpu.CompilerParams(collective_id=1, has_side_effects=True),
        name="scatter",
    )(sf, sb)


def on_device(integrals, block_lists, coeff, match, ex_blocks):
    nq, naux, occ = 3, 64, 256
    factor = -((nq * naux * occ) ** (-0.5))
    lists = block_lists[:, 0, 0]
    cells = lists[:, 0] * 16 + lists[:, 1]
    number = jnp.arange(144, dtype=jnp.int32).reshape(3, 1, 48)
    hit = cells[:, None, :] == jnp.arange(256, dtype=jnp.int32)[None, :, None]
    idx = jnp.min(jnp.where(hit, number, 144), axis=2)
    part = lax.dynamic_index_in_dim(match, lax.axis_index("ka"), axis=1, keepdims=False)
    g = gather(coeff).reshape(4, 2, 2, 1024, 128)
    sf, sb = local(idx, part, ex_blocks[0], integrals.reshape(144, 64, 128), g)
    return scatter(factor, sf, sb)[None]


def solution(mesh):
    return jax.shard_map(
        on_device,
        mesh=mesh,
        in_specs=(
            P(None, "ka", "fit", None, None, None),
            P(None, "ka", "fit", None, None),
            P("ka", None, "fit", None),
            P(),
            P("ka", None, None),
        ),
        out_specs=P("ka", "fit", None),
        check_vma=False,
    )
```

```python
import jax
import jax.numpy as jnp
from jax import lax
from jax.experimental import pallas as pl
from jax.experimental.pallas import tpu as pltpu
from jax.sharding import PartitionSpec as P

MESH = pl.DeviceIdType.MESH
NT = (((1,), (1,)), ((), ()))
F32 = jnp.float32
BF16 = jnp.bfloat16


def place():
    ka, fit = lax.axis_index("ka"), lax.axis_index("fit")
    x, y, zl = fit // 16, (fit // 4) % 4, fit % 4
    return ka // 2, ka % 2, x, y, zl


def device(zh, c, x, y, zl):
    return (zh * 2 + c, x * 16 + y * 4 + zl)


def rcopy(src, dst, ssem, rsem, dev):
    return pltpu.make_async_remote_copy(
        src_ref=src, dst_ref=dst, send_sem=ssem, recv_sem=rsem, device_id=dev, device_id_type=MESH
    )


def greet(devices):
    barrier = pltpu.get_barrier_semaphore()
    for dev in devices:
        pl.semaphore_signal(barrier, inc=1, device_id=dev, device_id_type=MESH)
    pl.semaphore_wait(barrier, len(devices))


def fused_kernel(factor, idx, match, ex, coeff, lin, out, *scratch):
    (ga, gb, ga_m, gb_m, ga_p, gb_p, ga_2, gb_2, lv, ld, xa, xs, sd, sf, sb, ra, rb, t, a1f, a1b, qa, qb, qt, a2f, a2b, zin, where) = scratch[:27]
    lsem, zs, zr, rs, rr, bs, br, ss, sr, ws, wr = scratch[27:]
    gs = ({0: ga, -1: ga_m, 1: ga_p, 2: ga_2}, {0: gb, -1: gb_m, 1: gb_p, 2: gb_2})
    zh, c, x, y, zl = place()
    z = zh * 4 + zl
    own = pl.ds(pl.multiple_of(zl * 16, 16), 16)
    loads = []
    for h in range(2):
        for s in range(2):
            cp = pltpu.make_async_copy(
                coeff.at[0, s, :, h * 128 : (h + 1) * 128],
                (ga.at[c * 2 + zh, s, y, own], gb.at[c * 2 + zh, s, x, own])[h],
                lsem.at[h * 2 + s],
            )
            cp.start()
            loads.append(cp)
    lcopy = pltpu.make_async_copy(lin, lv.at[0:144], lsem.at[4])
    lcopy.start()
    for k in range(4):
        where[k] = (k % 2) * 2 + k // 2

    def nb(dx, dy):
        return device(zh, c, (x + dx + 4) % 4, (y + dy + 4) % 4, zl)

    zdev = []
    for j in range(1, 8):
        zz = (z + j) % 8
        zdev.append(device(zz // 4, c, x, y, zz % 4))
    wdev = [device(zh, c, x, y, (zl + j) % 4) for j in range(1, 4)]
    sib = device(zh, 1 - c, x, y, zl)
    ax = (nb(1, 0), nb(-1, 0))
    ay = (nb(0, 1), nb(0, -1))
    greet(zdev + list(ax) + list(ay) + [sib])
    for cp in loads:
        cp.wait()

    mine = pl.ds(c * 2, 2)
    pieces = (ga.at[c * 2 + zh, :, y, own], gb.at[c * 2 + zh, :, x, own])
    zc = [rcopy(p, p, zs.at[j, h], zr.at[j, h], zdev[j]) for j in range(7) for h, p in enumerate(pieces)]
    for cp in zc:
        cp.start()

    lcopy.wait()
    lv[144] = jnp.zeros((64, 128), BF16)

    @pl.loop(0, 48)
    def _(i):
        q, cc = i // 16, i % 16
        for r in range(16):
            ld[q, cc, r * 64 : (r + 1) * 64, :] = lv[idx[q, r * 16 + cc]]

    for cp in zc:
        cp.wait()

    def ring(n, axis, src, dst):
        first = {}
        for s in range(2):
            for i in range(2):
                k = s if i == 0 else 1 - s
                cp = rcopy(src(k), dst[i](k), rs.at[n, i, k], rr.at[n, i, k], axis[i])
                cp.start()
                first[i, k] = cp
        return first

    def relay(n, axis, first, src, dst):
        cps = []
        for i in range(2):
            first[i, i].wait_recv()
            cp = rcopy(src[i](i), dst(i), rs.at[n, 2, i], rr.at[n, 2, i], axis[i])
            cp.start()
            cps.append(cp)
        return cps

    def row(h, d):
        return lambda k: gs[h][0].at[mine, k, ((y, x)[h] + d + 4) % 4]

    def whole(h, d):
        return lambda k: gs[h][d].at[mine, k]

    fa, fb = (ring(h, (ay, ax)[h], row(h, 0), [row(h, 0)] * 2) for h in range(2))
    ra2, rb2 = (
        relay(h, (ay, ax)[h], (fa, fb)[h], [row(h, -1), row(h, 1)], lambda k, h=h: row(h, (-1, 1)[k])(k))
        for h in range(2)
    )
    for f in (fa, fb):
        f[0, 1].wait_recv()
        f[1, 0].wait_recv()
    for cp in ra2 + rb2:
        cp.wait_recv()
    fa3, fb3 = (ring(2 + h, (ax, ay)[h], whole(h, 0), [whole(h, -1), whole(h, 1)]) for h in range(2))
    sibs = {}

    def to_sib(h, d):
        sibs[h, d] = []
        for k in range(2):
            ref = whole(h, d)(k)
            cp = rcopy(ref, ref, bs.at[h, d + 1, k], br.at[h, d + 1, k], sib)
            cp.start()
            sibs[h, d].append(cp)

    def from_sib(h, d):
        for cp in sibs[h, d]:
            cp.wait_recv()

    def chunk(h, d, first, last):
        j = ((x if h == 0 else y) + d + 4) % 4

        @pl.loop(0, 3)
        def _(q):
            pk = where[match[q, zh * 2 + c]]
            left, right = [], []
            for i in range(4):
                bx, by = (j, i) if h == 0 else (i, j)
                left.append(ld[q, bx * 4 + by])
                re, im = (gs[h][d][pk, s, i] for s in range(2))
                right += [jnp.concatenate([re, im], axis=1), jnp.concatenate([-im, re], axis=1)]
            v = jnp.dot(
                jnp.concatenate(left, axis=1), jnp.concatenate(right, axis=0), preferred_element_type=F32
            )
            if not first:
                v = v + xa[q, h]
            if last:
                xs[q, h] = v.astype(BF16)
            else:
                xa[q, h] = v

    to_sib(0, 0)
    to_sib(1, 0)
    for h in range(2):
        from_sib(h, 0)
        chunk(h, 0, True, False)
    ra3, rb3 = (
        relay(2 + h, (ax, ay)[h], (fa3, fb3)[h], [whole(h, -1), whole(h, 1)], whole(h, 2)) for h in range(2)
    )
    for f in (fa3, fb3):
        f[0, 1].wait_recv()
        f[1, 0].wait_recv()
    for d in (-1, 1):
        to_sib(0, d)
        to_sib(1, d)
    for h in range(2):
        from_sib(h, -1)
        chunk(h, -1, False, False)
    for cp in ra3 + rb3:
        cp.wait_recv()
    to_sib(0, 2)
    to_sib(1, 2)
    for h in range(2):
        from_sib(h, 1)
        chunk(h, 1, False, False)
    for h in range(2):
        from_sib(h, 2)
        chunk(h, 2, False, True)

    @pl.loop(0, 8)
    def _(i):
        cols = pl.ds(pl.multiple_of(i * 128, 128), 128)
        left, right = [], []
        for q in range(3):
            for h in range(2):
                b = xs[q, h, cols, :]
                w = jnp.concatenate([-b[:, 128:], b[:, :128]], axis=1)
                left.append(xs[q, h])
                right.append(jnp.concatenate([b[:64], w[:64], b[64:], w[64:]], axis=0))
        acc = lax.dot_general(left[0], right[0], NT, preferred_element_type=F32)
        for k in range(1, 6):
            acc += lax.dot_general(left[k], right[k], NT, preferred_element_type=F32)
        sd[2 * i] = acc[:, :128].reshape(16, 64, 128)
        sd[2 * i + 1] = acc[:, 128:].reshape(16, 64, 128)

    @pl.loop(0, 16)
    def _(i):
        for u in range(4):
            e = i * 4 + u
            v = sd[ex[1, e], ex[0, e]]
            for p in range(2):
                half = v[p * 32 : (p + 1) * 32]
                sf[p, i // 4, i % 4, u] = half
                sb[p, i // 4, i % 4, u] = half.astype(BF16)

    def begin(n, axis, blk, r1, r2):
        up, down = axis
        cps = [
            rcopy(blk(2, 0), r1.at[0], ss.at[n, 0], sr.at[n, 0], up),
            rcopy(blk(2, 1), r1.at[1], ss.at[n, 1], sr.at[n, 1], down),
            rcopy(blk(1, 1), r2.at[0], ss.at[n, 2], sr.at[n, 2], up),
            rcopy(blk(-1, 0), r2.at[1], ss.at[n, 3], sr.at[n, 3], down),
        ]
        for cp in cps:
            cp.start()
        return cps

    def middle(n, axis, first, val, r1, tmp, r3):
        cps = []
        for i in range(2):
            first[i].wait_recv()
            tmp[i] = (r1[i].astype(F32) + val((1, -1)[i], i)).astype(BF16)
            cp = rcopy(tmp.at[i], r3.at[i], ss.at[n, 4 + i], sr.at[n, 4 + i], axis[i])
            cp.start()
            cps.append(cp)
        return cps

    def pick1(ref, p):
        def f(d, i):
            j = ((x if p == 0 else y) + d + 4) % 4
            return ref.at[0, j, 2 * i : 2 * i + 2] if p == 0 else ref.at[1, 2 * i : 2 * i + 2, j]

        return f

    def pick2(ref, p):
        return lambda d, i: ref.at[p, ((y if p == 0 else x) + d + 4) % 4, 2 * i : 2 * i + 2]

    def stage(n, axes, fblk, bblk, r1, r2, r3, tmp):
        first = [begin(n + p, axes[p], bblk[p], r1.at[p], r2.at[p]) for p in range(2)]
        val = [lambda d, i, p=p: fblk[p](d, i)[...] for p in range(2)]
        mid = [middle(n + p, axes[p], first[p], val[p], r1.at[p], tmp.at[p], r3.at[p]) for p in range(2)]
        return first, mid, val

    def finish(first, mid, val, r2, r3, p, i):
        first[p][3 - i].wait_recv()
        mid[p][i].wait_recv()
        return val[p](0, i) + r2[p, 1 - i].astype(F32) + r3[p, i].astype(F32)

    f1, m1, v1 = stage(
        0, (ax, ay), [pick1(sf, p) for p in range(2)], [pick1(sb, p) for p in range(2)], ra.at[0], ra.at[1], rb, t
    )
    for p in range(2):
        for i in range(2):
            v = finish(f1, m1, v1, ra.at[1], rb, p, i)
            a1f[p, 2 * i : 2 * i + 2] = v
            a1b[p, 2 * i : 2 * i + 2] = v.astype(BF16)
    f2, m2, v2 = stage(
        2, (ay, ax), [pick2(a1f, p) for p in range(2)], [pick2(a1b, p) for p in range(2)], qa.at[0], qa.at[1], qb, qt
    )
    for p in range(2):
        for i in range(2):
            v = finish(f2, m2, v2, qa.at[1], qb, p, i)
            a2f[p, 2 * i : 2 * i + 2] = v
            a2b[p, 2 * i : 2 * i + 2] = v.astype(BF16)
    wc = []
    for j in range(3):
        cp = rcopy(a2b.at[:, (zl + j + 1) % 4], zin.at[j], ws.at[j], wr.at[j], wdev[j])
        cp.start()
        wc.append(cp)
    total = a2f[:, zl]
    for j in range(3):
        wc[j].wait_recv()
        total = total + zin[j].astype(F32)
    total = total * factor
    out[0:32] = total[0]
    out[32:64] = total[1]
    for f in (fa, fb, fa3, fb3):
        for cp in f.values():
            cp.wait_send()
    for cps in sibs.values():
        for cp in cps:
            cp.wait_send()
    for cps in [ra2, rb2, ra3, rb3, wc] + f1 + m1 + f2 + m2:
        for cp in cps:
            cp.wait_send()


def fused(factor, idx, match, ex, coeff, lin):
    smem = pl.BlockSpec(memory_space=pltpu.SMEM)
    vmem = pl.BlockSpec(memory_space=pltpu.VMEM)
    hbm = pl.BlockSpec(memory_space=pl.ANY)
    dma = pltpu.SemaphoreType.DMA
    half, quarter = (2, 4, 32, 128), (2, 32, 128)
    blocks = (2, 4, 4, 4, 32, 128)

    def kern(*refs):
        fused_kernel(factor, *refs)

    return pl.pallas_call(
        kern,
        out_shape=jax.ShapeDtypeStruct((64, 128), F32),
        in_specs=[smem] * 3 + [hbm] * 2,
        out_specs=vmem,
        scratch_shapes=[pltpu.VMEM((4, 2, 4, 64, 128), BF16)] * 8
        + [
            pltpu.VMEM((145, 64, 128), BF16),
            pltpu.VMEM((3, 16, 1024, 128), BF16),
            pltpu.VMEM((3, 2, 1024, 256), F32),
            pltpu.VMEM((3, 2, 1024, 256), BF16),
            pltpu.VMEM((16, 16, 64, 128), F32),
            pltpu.VMEM(blocks, F32),
            pltpu.VMEM(blocks, BF16),
            pltpu.VMEM((2, 2, 2) + half, BF16),
            pltpu.VMEM((2, 2) + half, BF16),
            pltpu.VMEM((2, 2) + half, BF16),
            pltpu.VMEM((2, 4, 4, 32, 128), F32),
            pltpu.VMEM((2, 4, 4, 32, 128), BF16),
            pltpu.VMEM((2, 2, 2) + quarter, BF16),
            pltpu.VMEM((2, 2) + quarter, BF16),
            pltpu.VMEM((2, 2) + quarter, BF16),
            pltpu.VMEM((2, 4, 32, 128), F32),
            pltpu.VMEM((2, 4, 32, 128), BF16),
            pltpu.VMEM((3, 2, 32, 128), BF16),
            pltpu.SMEM((4,), jnp.int32),
            dma((5,)),
            dma((7, 2)),
            dma((7, 2)),
            dma((4, 3, 2)),
            dma((4, 3, 2)),
            dma((2, 4, 2)),
            dma((2, 4, 2)),
            dma((4, 6)),
            dma((4, 6)),
            dma((3,)),
            dma((3,)),
        ],
        compiler_params=pltpu.CompilerParams(
            collective_id=0, has_side_effects=True, vmem_limit_bytes=60 * 2**20
        ),
        name="fused",
    )(idx, match, ex, coeff, lin)


def on_device(integrals, block_lists, coeff, match, ex_blocks):
    nq, naux, occ = 3, 64, 256
    factor = -((nq * naux * occ) ** (-0.5))
    lists = block_lists[:, 0, 0]
    cells = lists[:, 0] * 16 + lists[:, 1]
    number = jnp.arange(144, dtype=jnp.int32).reshape(3, 1, 48)
    hit = cells[:, None, :] == jnp.arange(256, dtype=jnp.int32)[None, :, None]
    idx = jnp.min(jnp.where(hit, number, 144), axis=2)
    lin = integrals.reshape(144, 64, 128)
    return fused(factor, idx, match, ex_blocks[0], coeff, lin)[None]


def solution(mesh):
    return jax.shard_map(
        on_device,
        mesh=mesh,
        in_specs=(
            P(None, "ka", "fit", None, None, None),
            P(None, "ka", "fit", None, None),
            P("ka", None, "fit", None),
            P(),
            P("ka", None, None),
        ),
        out_specs=P("ka", "fit", None),
        check_vma=False,
    )
```

```python
import jax
import jax.numpy as jnp
from jax import lax
from jax.experimental import pallas as pl
from jax.experimental.pallas import tpu as pltpu
from jax.sharding import PartitionSpec as P

MESH = pl.DeviceIdType.MESH
NT = (((1,), (1,)), ((), ()))
F32 = jnp.float32
BF16 = jnp.bfloat16


def place():
    ka, fit = lax.axis_index("ka"), lax.axis_index("fit")
    x, y, zl = fit // 16, (fit // 4) % 4, fit % 4
    return ka // 2, ka % 2, x, y, zl


def device(zh, c, x, y, zl):
    return (zh * 2 + c, x * 16 + y * 4 + zl)


def rcopy(src, dst, ssem, rsem, dev):
    return pltpu.make_async_remote_copy(
        src_ref=src, dst_ref=dst, send_sem=ssem, recv_sem=rsem, device_id=dev, device_id_type=MESH
    )


def greet(devices):
    barrier = pltpu.get_barrier_semaphore()
    for dev in devices:
        pl.semaphore_signal(barrier, inc=1, device_id=dev, device_id_type=MESH)
    pl.semaphore_wait(barrier, len(devices))


def fused_kernel(factor, match, ex, lists, coeff, lin, out, *scratch):
    (ga, gb, ga_m, gb_m, ga_p, gb_p, ga_2, gb_2, lv, ld, xa, xs, sf, sb, rin, acc, zb, zin, table, where, idx) = scratch[:21]
    lsem, zs, zr, ps, pr, rs, rr, bs, br, ss, sr, ws, wr = scratch[21:]
    gs = ({0: ga, -1: ga_m, 1: ga_p, 2: ga_2}, {0: gb, -1: gb_m, 1: gb_p, 2: gb_2})
    zh, c, x, y, zl = place()
    z = zh * 4 + zl
    own = pl.ds(pl.multiple_of(zl * 16, 16), 16)
    loads = []
    for h in range(2):
        for s in range(2):
            cp = pltpu.make_async_copy(
                coeff.at[0, s, :, h * 128 : (h + 1) * 128],
                (ga.at[c * 2 + zh, s, y, own], gb.at[c * 2 + zh, s, x, own])[h],
                lsem.at[h * 2 + s],
            )
            cp.start()
            loads.append(cp)
    lcopy = pltpu.make_async_copy(lin, lv.at[0:144], lsem.at[4])
    lcopy.start()
    same = lax.broadcasted_iota(jnp.int32, (48, 48), 0) == lax.broadcasted_iota(jnp.int32, (48, 48), 1)
    for q in range(3):
        cells = lists[q, 0:1, :] * 16 + lists[q, 1:2, :]
        cells = jnp.sum(jnp.where(same, jnp.broadcast_to(cells, (48, 48)), 0), axis=1, keepdims=True)
        hit = jnp.broadcast_to(cells, (48, 256)) == lax.broadcasted_iota(jnp.int32, (48, 256), 1)
        number = lax.broadcasted_iota(jnp.int32, (48, 256), 0) + (q * 48 - 144)
        found = jnp.sum(jnp.where(hit, number, 0), axis=0, keepdims=True) + 144
        table[q : q + 1, :] = jnp.maximum(found, 0)
    tcopy = pltpu.make_async_copy(table, idx, lsem.at[5])
    tcopy.start()
    for k in range(4):
        where[k] = (k % 2) * 2 + k // 2

    def nb(dx, dy):
        return device(zh, c, (x + dx + 4) % 4, (y + dy + 4) % 4, zl)

    zdev = []
    for j in range(1, 8):
        zz = (z + j) % 8
        zdev.append(device(zz // 4, c, x, y, zz % 4))
    wdev = [device(zh, c, x, y, (zl + j) % 4) for j in range(1, 4)]
    sib = device(zh, 1 - c, x, y, zl)
    ax = (nb(1, 0), nb(-1, 0))
    ay = (nb(0, 1), nb(0, -1))
    plane = [nb(dx, dy) for dx in range(4) for dy in range(4) if dx or dy]
    greet(zdev + plane + [sib])
    for cp in loads:
        cp.wait()

    mine = pl.ds(c * 2, 2)
    pieces = (ga.at[c * 2 + zh, :, y, own], gb.at[c * 2 + zh, :, x, own])
    zc = [rcopy(p, p, zs.at[j, h], zr.at[j, h], zdev[j]) for j in range(7) for h, p in enumerate(pieces)]
    for cp in zc:
        cp.start()

    lcopy.wait()
    tcopy.wait()
    lv[144] = jnp.zeros((64, 128), BF16)

    @pl.loop(0, 48)
    def _(i):
        q, cc = i // 16, i % 16
        for r in range(16):
            ld[q, cc, r * 64 : (r + 1) * 64, :] = lv[idx[q, r * 16 + cc]]

    for cp in zc:
        cp.wait()

    def ring(n, axis, src, dst):
        first = {}
        for s in range(2):
            for i in range(2):
                k = s if i == 0 else 1 - s
                cp = rcopy(src(k), dst[i](k), rs.at[n, i, k], rr.at[n, i, k], axis[i])
                cp.start()
                first[i, k] = cp
        return first

    def relay(n, axis, first, src, dst):
        cps = []
        for i in range(2):
            first[i, i].wait_recv()
            cp = rcopy(src[i](i), dst(i), rs.at[n, 2, i], rr.at[n, 2, i], axis[i])
            cp.start()
            cps.append(cp)
        return cps

    def whole(h, d):
        return lambda k: gs[h][d].at[mine, k]

    pc = []
    for d in range(1, 4):
        for h in range(2):
            ref = gs[h][0].at[mine, :, (y, x)[h]]
            cp = rcopy(ref, ref, ps.at[h, d - 1], pr.at[h, d - 1], (nb(0, d), nb(d, 0))[h])
            cp.start()
            pc.append(cp)
    for cp in pc:
        cp.wait_recv()
    fa3, fb3 = (ring(h, (ax, ay)[h], whole(h, 0), [whole(h, -1), whole(h, 1)]) for h in range(2))
    sibs = {}

    def to_sib(h, d):
        sibs[h, d] = []
        for k in range(2):
            ref = whole(h, d)(k)
            cp = rcopy(ref, ref, bs.at[h, d + 1, k], br.at[h, d + 1, k], sib)
            cp.start()
            sibs[h, d].append(cp)

    def from_sib(h, d):
        for cp in sibs[h, d]:
            cp.wait_recv()

    def chunk(h, d, first, last):
        j = ((x if h == 0 else y) + d + 4) % 4

        @pl.loop(0, 3)
        def _(q):
            pk = where[match[q, zh * 2 + c]]
            left, right = [], []
            for i in range(4):
                bx, by = (j, i) if h == 0 else (i, j)
                left.append(ld[q, bx * 4 + by])
                re, im = (gs[h][d][pk, s, i] for s in range(2))
                right += [jnp.concatenate([re, im], axis=1), jnp.concatenate([-im, re], axis=1)]
            v = jnp.dot(
                jnp.concatenate(left, axis=1), jnp.concatenate(right, axis=0), preferred_element_type=F32
            )
            if not first:
                v = v + xa[q, h]
            if last:
                xs[q, h] = v.astype(BF16).reshape(16, 64, 256)
            else:
                xa[q, h] = v

    to_sib(0, 0)
    to_sib(1, 0)
    for h in range(2):
        from_sib(h, 0)
        chunk(h, 0, True, False)
    ra3, rb3 = (
        relay(h, (ax, ay)[h], (fa3, fb3)[h], [whole(h, -1), whole(h, 1)], whole(h, 2)) for h in range(2)
    )
    for f in (fa3, fb3):
        f[0, 1].wait_recv()
        f[1, 0].wait_recv()
    for d in (-1, 1):
        to_sib(0, d)
        to_sib(1, d)
    for h in range(2):
        from_sib(h, -1)
        chunk(h, -1, False, False)
    for cp in ra3 + rb3:
        cp.wait_recv()
    to_sib(0, 2)
    to_sib(1, 2)
    for h in range(2):
        from_sib(h, 1)
        chunk(h, 1, False, False)
    for h in range(2):
        from_sib(h, 2)
        chunk(h, 2, False, True)

    def column(dx, dy):
        return (x + dx) % 4, (y + dy) % 4

    def send(i, jj):
        cx, cy = column((i + 1) % 4, (i + 1 + jj) % 4)
        slot = jj * 4 + i
        return rcopy(sb.at[slot], rin.at[slot], ss.at[slot], sr.at[slot], device(zh, c, cx, cy, zl))

    @pl.loop(0, 4)
    def _(jj):
        for i in range(4):
            cx, cy = column((i + 1) % 4, (i + 1 + jj) % 4)
            for u in range(4):
                e = (cx * 4 + cy) * 4 + u
                r, s = ex[0, e], ex[1, e]
                left, right = [], []
                for q in range(3):
                    for h in range(2):
                        a = xs[q, h, r]
                        left.append(
                            jnp.concatenate([a, jnp.concatenate([a[:, 128:], -a[:, :128]], axis=1)], axis=0)
                        )
                        right.append(xs[q, h, s])
                v = lax.dot_general(
                    jnp.concatenate(left, axis=1), jnp.concatenate(right, axis=1), NT, preferred_element_type=F32
                )
                v = jnp.concatenate([v[:64], v[64:]], axis=1)
                sb[jj * 4 + i, u] = v.astype(BF16)
                if i == 3:
                    sf[jj, u] = v
            if i < 3:
                send(i, jj).start()
            else:

                @pl.when(jj > 0)
                def _():
                    send(3, jj).start()

    acc[...] = sf[0]
    sent = []
    for jj in range(4):
        for i in range(4):
            if i == 3 and jj == 0:
                continue
            cp = send(i, jj)
            sent.append(cp)
            cp.wait_recv()
            acc[...] += rin[jj * 4 + i].astype(F32)
    zb[...] = acc[...].astype(BF16)
    wc = []
    for j in range(3):
        cp = rcopy(zb.at[(zl + j + 1) % 4], zin.at[j], ws.at[j], wr.at[j], wdev[j])
        cp.start()
        wc.append(cp)
    total = acc[zl]
    for j in range(3):
        wc[j].wait_recv()
        total = total + zin[j].astype(F32)
    out[...] = total * factor
    for f in (fa3, fb3):
        for cp in f.values():
            cp.wait_send()
    for cps in sibs.values():
        for cp in cps:
            cp.wait_send()
    for cp in pc + ra3 + rb3 + sent + wc:
        cp.wait_send()


def fused(factor, match, ex, lists, coeff, lin):
    smem = pl.BlockSpec(memory_space=pltpu.SMEM)
    vmem = pl.BlockSpec(memory_space=pltpu.VMEM)
    hbm = pl.BlockSpec(memory_space=pl.ANY)
    dma = pltpu.SemaphoreType.DMA

    def kern(*refs):
        fused_kernel(factor, *refs)

    return pl.pallas_call(
        kern,
        out_shape=jax.ShapeDtypeStruct((64, 128), F32),
        in_specs=[smem] * 2 + [vmem] + [hbm] * 2,
        out_specs=vmem,
        scratch_shapes=[pltpu.VMEM((4, 2, 4, 64, 128), BF16)] * 8
        + [
            pltpu.VMEM((145, 64, 128), BF16),
            pltpu.VMEM((3, 16, 1024, 128), BF16),
            pltpu.VMEM((3, 2, 1024, 256), F32),
            pltpu.VMEM((3, 2, 16, 64, 256), BF16),
            pltpu.VMEM((4, 4, 64, 128), F32),
            pltpu.VMEM((16, 4, 64, 128), BF16),
            pltpu.VMEM((16, 4, 64, 128), BF16),
            pltpu.VMEM((4, 64, 128), F32),
            pltpu.VMEM((4, 64, 128), BF16),
            pltpu.VMEM((3, 64, 128), BF16),
            pltpu.VMEM((3, 256), jnp.int32),
            pltpu.SMEM((4,), jnp.int32),
            pltpu.SMEM((3, 256), jnp.int32),
            dma((6,)),
            dma((7, 2)),
            dma((7, 2)),
            dma((2, 3)),
            dma((2, 3)),
            dma((2, 3, 2)),
            dma((2, 3, 2)),
            dma((2, 4, 2)),
            dma((2, 4, 2)),
            dma((16,)),
            dma((16,)),
            dma((3,)),
            dma((3,)),
        ],
        compiler_params=pltpu.CompilerParams(
            collective_id=0, has_side_effects=True, vmem_limit_bytes=60 * 2**20
        ),
        name="fused",
    )(match, ex, lists, coeff, lin)


def on_device(integrals, block_lists, coeff, match, ex_blocks):
    nq, naux, occ = 3, 64, 256
    factor = -((nq * naux * occ) ** (-0.5))
    lin = integrals.reshape(144, 64, 128)
    return fused(factor, match, ex_blocks[0], block_lists[:, 0, 0], coeff, lin)[None]


def solution(mesh):
    return jax.shard_map(
        on_device,
        mesh=mesh,
        in_specs=(
            P(None, "ka", "fit", None, None, None),
            P(None, "ka", "fit", None, None),
            P("ka", None, "fit", None),
            P(),
            P("ka", None, None),
        ),
        out_specs=P("ka", "fit", None),
        check_vma=False,
    )
```

```python
import jax
import jax.numpy as jnp
from jax import lax
from jax.experimental import pallas as pl
from jax.experimental.pallas import tpu as pltpu
from jax.sharding import PartitionSpec as P

MESH = pl.DeviceIdType.MESH
NT = (((1,), (1,)), ((), ()))
F32 = jnp.float32
BF16 = jnp.bfloat16


def place():
    ka, fit = lax.axis_index("ka"), lax.axis_index("fit")
    x, y, zl = fit // 16, (fit // 4) % 4, fit % 4
    return ka // 2, ka % 2, x, y, zl


def device(zh, c, x, y, zl):
    return (zh * 2 + c, x * 16 + y * 4 + zl)


def rcopy(src, dst, ssem, rsem, dev):
    return pltpu.make_async_remote_copy(
        src_ref=src, dst_ref=dst, send_sem=ssem, recv_sem=rsem, device_id=dev, device_id_type=MESH
    )


def greet(devices):
    barrier = pltpu.get_barrier_semaphore()
    for dev in devices:
        pl.semaphore_signal(barrier, inc=1, device_id=dev, device_id_type=MESH)
    pl.semaphore_wait(barrier, len(devices))


def fused_kernel(factor, match, ex, lists, coeff, lin, out, *scratch):
    own, far = scratch[0:2], scratch[2:14]
    (lv, ld, xa, xs, sf, sb, rin, af, ab, qin, cf, cb, zin, table, where, idx) = scratch[14:30]
    lsem, zs, zr, ps, pr, rs, rr, bs, br, ss, sr, qs, qr, ws, wr = scratch[30:]
    zh, c, x, y, zl = place()
    z = zh * 4 + zl
    cell = (y, x)
    mine = pl.ds(c * 2, 2)
    dist = {-1: 0, 1: 1, 2: 2}
    loads = []
    for h in range(2):
        for s in range(2):
            cp = pltpu.make_async_copy(
                coeff.at[0, s, :, h * 128 : (h + 1) * 128],
                own[h].at[c * 2 + zh, cell[h], zl, s],
                lsem.at[h * 2 + s],
            )
            cp.start()
            loads.append(cp)
    lcopy = pltpu.make_async_copy(lin, lv.at[0:144], lsem.at[4])
    lcopy.start()

    def nb(dx, dy):
        return device(zh, c, (x + dx + 4) % 4, (y + dy + 4) % 4, zl)

    def cross(h, d):
        return (nb(0, d), nb(d, 0))[h]

    def along(h, d):
        return (nb(d, 0), nb(0, d))[h]

    zdev = []
    for j in range(1, 8):
        zz = (z + j) % 8
        zdev.append(device(zz // 4, c, x, y, zz % 4))
    wdev = [device(zh, c, x, y, (zl + j) % 4) for j in range(1, 4)]
    sib = device(zh, 1 - c, x, y, zl)
    greet(zdev + [f(0, d) for f in (cross, along) for d in range(1, 4)] + [sib])
    for cp in loads:
        cp.wait()

    zc = []
    for j in range(7):
        for h in range(2):
            ref = own[h].at[c * 2 + zh, cell[h], zl]
            cp = rcopy(ref, ref, zs.at[j, h], zr.at[j, h], zdev[j])
            cp.start()
            zc.append(cp)

    same = lax.broadcasted_iota(jnp.int32, (48, 48), 0) == lax.broadcasted_iota(jnp.int32, (48, 48), 1)
    for q in range(3):
        cells = lists[q, 0:1, :] * 16 + lists[q, 1:2, :]
        cells = jnp.sum(jnp.where(same, jnp.broadcast_to(cells, (48, 48)), 0), axis=1, keepdims=True)
        hit = jnp.broadcast_to(cells, (48, 256)) == lax.broadcasted_iota(jnp.int32, (48, 256), 1)
        number = lax.broadcasted_iota(jnp.int32, (48, 256), 0) + (q * 48 - 144)
        found = jnp.sum(jnp.where(hit, number, 0), axis=0, keepdims=True) + 144
        table[q : q + 1, :] = jnp.maximum(found, 0)
    tcopy = pltpu.make_async_copy(table, idx, lsem.at[5])
    tcopy.start()
    for k in range(4):
        where[k] = (k % 2) * 2 + k // 2
    lcopy.wait()
    lv[144] = jnp.zeros((64, 128), BF16)
    tcopy.wait()

    @pl.loop(0, 48)
    def _(i):
        q, cc = i // 16, i % 16
        for r in range(16):
            ld[q, cc, r * 64 : (r + 1) * 64, :] = lv[idx[q, r * 16 + cc]]

    for cp in zc:
        cp.wait()

    pc = []
    for d in range(1, 4):
        for h in range(2):
            ref = own[h].at[mine, cell[h]]
            cp = rcopy(ref, ref, ps.at[h, d - 1], pr.at[h, d - 1], cross(h, d))
            cp.start()
            pc.append(cp)
    for cp in pc:
        cp.wait_recv()

    def buf(h, d, k):
        return far[(h * 3 + dist[d]) * 2 + k]

    first, sibs, relays = {}, {}, []
    for s in range(2):
        for h in range(2):
            for i, d in enumerate((1, -1)):
                k = s if i == 0 else 1 - s
                cp = rcopy(
                    own[h].at[mine, 2 * k : 2 * k + 2],
                    buf(h, -d, k).at[mine],
                    rs.at[h, i, k],
                    rr.at[h, i, k],
                    along(h, d),
                )
                cp.start()
                first[h, i, k] = cp

    def to_sib(h, ref, n):
        cp = rcopy(ref.at[mine], ref.at[mine], bs.at[h, n], br.at[h, n], sib)
        cp.start()
        sibs[h, n] = cp

    def to_sib_far(h, d, k):
        to_sib(h, buf(h, d, k), 1 + dist[d] * 2 + k)

    def chunk(h, parts, begin, end):
        @pl.loop(0, 3)
        def _(q):
            pk = where[match[q, zh * 2 + c]]
            left, right = [], []
            for ref, n, i, d in parts:
                j = ((x, y)[h] + d + 4) % 4
                left.append(ld[q, j * 4 + i] if h == 0 else ld[q, i * 4 + j])
                re, im = (ref[pk, n, :, s].reshape(64, 128) for s in range(2))
                right += [jnp.concatenate([re, im], axis=1), jnp.concatenate([-im, re], axis=1)]
            v = jnp.dot(
                jnp.concatenate(left, axis=1), jnp.concatenate(right, axis=0), preferred_element_type=F32
            )
            if not begin:
                v = v + xa[q, h]
            if end:
                xs[q, h] = v.astype(BF16).reshape(16, 64, 256)
            else:
                xa[q, h] = v

    def far_chunk(h, pairs, end=False):
        for d, k in pairs:
            sibs[h, 1 + dist[d] * 2 + k].wait_recv()
        chunk(h, [(buf(h, d, k), n, 2 * k + n, d) for d, k in pairs for n in range(2)], False, end)

    for h in range(2):
        to_sib(h, own[h], 0)
    for h in range(2):
        sibs[h, 0].wait_recv()
        chunk(h, [(own[h], i, i, 0) for i in range(4)], True, False)
    early, late, last = ((-1, 0), (1, 1)), ((-1, 1), (1, 0)), ((2, 0), (2, 1))
    for h in range(2):
        for i, (d, k) in enumerate(early):
            first[h, i, k].wait_recv()
            cp = rcopy(buf(h, d, k).at[mine], buf(h, 2, k).at[mine], rs.at[h, 2, k], rr.at[h, 2, k], along(h, -d))
            cp.start()
            relays.append(cp)
            to_sib_far(h, d, k)
    far_chunk(0, early)
    for h in range(2):
        for i, (d, k) in enumerate(late):
            first[h, i, k].wait_recv()
            to_sib_far(h, d, k)
    far_chunk(1, early)
    far_chunk(0, late)
    for n, (h, k) in enumerate(((0, 0), (0, 1), (1, 0), (1, 1))):
        relays[n].wait_recv()
        to_sib_far(h, 2, k)
    far_chunk(1, late)
    far_chunk(0, last, True)
    far_chunk(1, last, True)

    def distance(o):
        return (1 - o // 2) * (2 - o) + (o // 2) * (9 - 3 * o)

    def send(p, o):
        d = distance(o)
        return rcopy(sb.at[p, o], rin.at[p, o], ss.at[p, o], sr.at[p, o], along(p, d))

    @pl.loop(0, 4)
    def _(o):
        d = distance(o)
        for p in range(2):
            j = ((x, y)[p] + d) % 4
            for i in range(4):
                for u in range(2):
                    e = ((j * 4 + i) if p == 0 else (i * 4 + j)) * 4 + 2 * p + u
                    r, s = ex[0, e], ex[1, e]
                    left, right = [], []
                    for q in range(3):
                        for h in range(2):
                            a = xs[q, h, r]
                            left.append(
                                jnp.concatenate([a, jnp.concatenate([a[:, 128:], -a[:, :128]], axis=1)], axis=0)
                            )
                            right.append(xs[q, h, s])
                    v = lax.dot_general(
                        jnp.concatenate(left, axis=1),
                        jnp.concatenate(right, axis=1),
                        NT,
                        preferred_element_type=F32,
                    )
                    v = jnp.concatenate([v[:64], v[64:]], axis=1)
                    sb[p, o, i, u] = v.astype(BF16)
                    sf[p, i, u] = v

            @pl.when(o < 3)
            def _():
                send(p, o).start()

    sent = []
    for p in range(2):
        total = sf[p]
        for o in range(3):
            cp = send(p, o)
            sent.append(cp)
            cp.wait_recv()
            total = total + rin[p, o].astype(F32)
        af[p] = total
        ab[p] = total.astype(BF16)
        for d in range(1, 4):
            cp = rcopy(
                ab.at[p, (cell[p] + d) % 4], qin.at[p, d - 1], qs.at[p, d - 1], qr.at[p, d - 1], cross(p, d)
            )
            cp.start()
            sent.append(cp)
    for p in range(2):
        total = af[p, cell[p]]
        for d in range(1, 4):
            sent[p * 6 + 2 + d].wait_recv()
            total = total + qin[p, d - 1].astype(F32)
        cf[2 * p : 2 * p + 2] = total
        cb[2 * p : 2 * p + 2] = total.astype(BF16)
    wc = []
    for j in range(3):
        cp = rcopy(cb.at[(zl + j + 1) % 4], zin.at[j], ws.at[j], wr.at[j], wdev[j])
        cp.start()
        wc.append(cp)
    total = cf[zl]
    for j in range(3):
        wc[j].wait_recv()
        total = total + zin[j].astype(F32)
    out[...] = total * factor
    for cps in (first, sibs):
        for cp in cps.values():
            cp.wait_send()
    for cp in pc + relays + sent + wc:
        cp.wait_send()


def fused(factor, match, ex, lists, coeff, lin):
    smem = pl.BlockSpec(memory_space=pltpu.SMEM)
    vmem = pl.BlockSpec(memory_space=pltpu.VMEM)
    hbm = pl.BlockSpec(memory_space=pl.ANY)
    dma = pltpu.SemaphoreType.DMA

    def kern(*refs):
        fused_kernel(factor, *refs)

    scratch = [pltpu.VMEM((4, 4, 4, 2, 16, 128), BF16)] * 2 + [pltpu.VMEM((4, 2, 4, 2, 16, 128), BF16)] * 12
    scratch += [
        pltpu.VMEM((145, 64, 128), BF16),
        pltpu.VMEM((3, 16, 1024, 128), BF16),
        pltpu.VMEM((3, 2, 1024, 256), F32),
        pltpu.VMEM((3, 2, 16, 64, 256), BF16),
        pltpu.VMEM((2, 4, 2, 64, 128), F32),
        pltpu.VMEM((2, 4, 4, 2, 64, 128), BF16),
        pltpu.VMEM((2, 3, 4, 2, 64, 128), BF16),
        pltpu.VMEM((2, 4, 2, 64, 128), F32),
        pltpu.VMEM((2, 4, 2, 64, 128), BF16),
        pltpu.VMEM((2, 3, 2, 64, 128), BF16),
        pltpu.VMEM((4, 64, 128), F32),
        pltpu.VMEM((4, 64, 128), BF16),
        pltpu.VMEM((3, 64, 128), BF16),
        pltpu.VMEM((3, 256), jnp.int32),
        pltpu.SMEM((4,), jnp.int32),
        pltpu.SMEM((3, 256), jnp.int32),
        dma((6,)),
    ]
    for shape in ((7, 2), (2, 3), (2, 3, 2), (2, 7), (2, 3), (2, 3), (3,)):
        scratch += [dma(shape)] * 2
    return pl.pallas_call(
        kern,
        out_shape=jax.ShapeDtypeStruct((64, 128), F32),
        in_specs=[smem] * 2 + [vmem] + [hbm] * 2,
        out_specs=vmem,
        scratch_shapes=scratch,
        compiler_params=pltpu.CompilerParams(
            collective_id=0, has_side_effects=True, vmem_limit_bytes=60 * 2**20
        ),
        name="fused",
    )(match, ex, lists, coeff, lin)


def on_device(integrals, block_lists, coeff, match, ex_blocks):
    nq, naux, occ = 3, 64, 256
    factor = -((nq * naux * occ) ** (-0.5))
    lin = integrals.reshape(144, 64, 128)
    return fused(factor, match, ex_blocks[0], block_lists[:, 0, 0], coeff, lin)[None]


def solution(mesh):
    return jax.shard_map(
        on_device,
        mesh=mesh,
        in_specs=(
            P(None, "ka", "fit", None, None, None),
            P(None, "ka", "fit", None, None),
            P("ka", None, "fit", None),
            P(),
            P("ka", None, None),
        ),
        out_specs=P("ka", "fit", None),
        check_vma=False,
    )
```

```python
import jax
import jax.numpy as jnp
from jax import lax
from jax.experimental import pallas as pl
from jax.experimental.pallas import tpu as pltpu
from jax.sharding import PartitionSpec as P

MESH = pl.DeviceIdType.MESH
NT = (((1,), (1,)), ((), ()))
F32 = jnp.float32
BF16 = jnp.bfloat16


def place():
    ka, fit = lax.axis_index("ka"), lax.axis_index("fit")
    x, y, zl = fit // 16, (fit // 4) % 4, fit % 4
    return ka // 2, ka % 2, x, y, zl


def device(zh, c, x, y, zl):
    return (zh * 2 + c, x * 16 + y * 4 + zl)


def rcopy(src, dst, ssem, rsem, dev):
    return pltpu.make_async_remote_copy(
        src_ref=src, dst_ref=dst, send_sem=ssem, recv_sem=rsem, device_id=dev, device_id_type=MESH
    )


def greet(devices):
    barrier = pltpu.get_barrier_semaphore()
    for dev in devices:
        pl.semaphore_signal(barrier, inc=1, device_id=dev, device_id_type=MESH)
    pl.semaphore_wait(barrier, len(devices))


def fused_kernel(factor, match, ex, lists, coeff, lin, out, *scratch):
    own, far = scratch[0:2], scratch[2:10]
    (lv, ld, xa, xs, sf, sb, rin, af, ab, qin, cf, cb, zin, table, where, idx) = scratch[10:26]
    lsem, zs, zr, ps, pr, rs, rr, bs, br, ss, sr, qs, qr, ws, wr = scratch[26:]
    groups = (
        ((-1, 0), (1, 0), (-1, 1), (1, 3)),
        ((-1, 3), (-1, 2), (1, 2), (1, 1)),
        ((2, 0), (2, 3)),
        ((2, 1), (2, 2)),
    )
    spot = {dr: (g, n) for g, drs in enumerate(groups) for n, dr in enumerate(drs)}
    zh, c, x, y, zl = place()
    z = zh * 4 + zl
    cell = (y, x)
    mine = pl.ds(c * 2, 2)
    loads = []
    for h in range(2):
        for s in range(2):
            cp = pltpu.make_async_copy(
                coeff.at[0, s, :, h * 128 : (h + 1) * 128],
                own[h].at[c * 2 + zh, 0, zl, s],
                lsem.at[h * 2 + s],
            )
            cp.start()
            loads.append(cp)
    lcopy = pltpu.make_async_copy(lin, lv.at[0:144], lsem.at[4])
    lcopy.start()

    def nb(dx, dy):
        return device(zh, c, (x + dx + 4) % 4, (y + dy + 4) % 4, zl)

    def cross(h, d):
        return (nb(0, d), nb(d, 0))[h]

    def along(h, d):
        return (nb(d, 0), nb(0, d))[h]

    zdev = []
    for j in range(1, 8):
        zz = (z + j) % 8
        zdev.append(device(zz // 4, c, x, y, zz % 4))
    wdev = [device(zh, c, x, y, (zl + j) % 4) for j in range(1, 4)]
    sib = device(zh, 1 - c, x, y, zl)
    greet(zdev + [f(0, d) for f in (cross, along) for d in range(1, 4)] + [sib])
    for cp in loads:
        cp.wait()

    zc = []
    for j in range(7):
        for h in range(2):
            ref = own[h].at[c * 2 + zh, 0, zl]
            cp = rcopy(ref, ref, zs.at[j, h], zr.at[j, h], zdev[j])
            cp.start()
            zc.append(cp)

    same = lax.broadcasted_iota(jnp.int32, (48, 48), 0) == lax.broadcasted_iota(jnp.int32, (48, 48), 1)
    for q in range(3):
        cells = lists[q, 0:1, :] * 16 + lists[q, 1:2, :]
        cells = jnp.sum(jnp.where(same, jnp.broadcast_to(cells, (48, 48)), 0), axis=1, keepdims=True)
        hit = jnp.broadcast_to(cells, (48, 256)) == lax.broadcasted_iota(jnp.int32, (48, 256), 1)
        number = lax.broadcasted_iota(jnp.int32, (48, 256), 0) + (q * 48 - 144)
        found = jnp.sum(jnp.where(hit, number, 0), axis=0, keepdims=True) + 144
        table[q : q + 1, :] = jnp.maximum(found, 0)
    tcopy = pltpu.make_async_copy(table, idx, lsem.at[5])
    tcopy.start()
    for k in range(4):
        where[k] = (k % 2) * 2 + k // 2
    lcopy.wait()
    lv[144] = jnp.zeros((64, 128), BF16)
    tcopy.wait()

    @pl.loop(0, 48)
    def _(i):
        q, cc = i // 16, i % 16
        for r in range(16):
            ld[q, cc, r * 64 : (r + 1) * 64, :] = lv[idx[q, r * 16 + cc]]

    for cp in zc:
        cp.wait()

    pc = []
    for d in range(1, 4):
        for h in range(2):
            cp = rcopy(
                own[h].at[mine, 0], own[h].at[mine, 4 - d], ps.at[h, d - 1], pr.at[h, d - 1], cross(h, d)
            )
            cp.start()
            pc.append(cp)

    def place_of(h, d, r):
        g, n = spot[d, r]
        return far[h * 4 + g].at[mine, n]

    moved, sibs = {}, {}

    def step(h, i, r):
        d = (1, -1)[i]
        cp = rcopy(own[h].at[mine, r], place_of(h, -d, r), rs.at[h, i, r], rr.at[h, i, r], along(h, d))
        cp.start()
        moved[h, i, r] = cp

    def relay(h, i, r, n):
        d = (1, -1)[i]
        moved[h, i, r].wait_recv()
        cp = rcopy(place_of(h, -d, r), place_of(h, 2, r), rs.at[h, i, n], rr.at[h, i, n], along(h, d))
        cp.start()
        moved[h, i, n] = cp

    def to_sib(h, ref, n):
        cp = rcopy(ref.at[mine], ref.at[mine], bs.at[h, n], br.at[h, n], sib)
        cp.start()
        sibs[h, n] = cp

    def chunk(h, cells, begin, end):
        @pl.loop(0, 3)
        def _(q):
            pk = where[match[q, zh * 2 + c]]
            left, right = [], []
            for ref, n, d, r in cells:
                j, i = ((x, y)[h] + d + 4) % 4, (cell[h] + r) % 4
                left.append(ld[q, j * 4 + i] if h == 0 else ld[q, i * 4 + j])
                re, im = (ref[pk, n, :, s].reshape(64, 128) for s in range(2))
                right += [jnp.concatenate([re, im], axis=1), jnp.concatenate([-im, re], axis=1)]
            v = jnp.dot(
                jnp.concatenate(left, axis=1), jnp.concatenate(right, axis=0), preferred_element_type=F32
            )
            if not begin:
                v = v + xa[q, h]
            if end:
                xs[q, h] = v.astype(BF16).reshape(16, 64, 256)
            else:
                xa[q, h] = v

    def far_chunk(h, g):
        sibs[h, 1 + g].wait_recv()
        chunk(h, [(far[h * 4 + g], n, d, r) for n, (d, r) in enumerate(groups[g])], False, g == 3)

    for h in range(2):
        step(h, 0, 0)
        step(h, 1, 0)
    for cp in pc:
        cp.wait_recv()
    for ru, rd in ((1, 3), (3, 2), (2, 1)):
        for h in range(2):
            step(h, 0, ru)
            step(h, 1, rd)
    for h in range(2):
        to_sib(h, own[h], 0)
    for h in range(2):
        relay(h, 0, 0, 4)
    for h in range(2):
        sibs[h, 0].wait_recv()
        chunk(h, [(own[h], r, 0, r) for r in range(4)], True, False)
    for h in range(2):
        relay(h, 1, 3, 4)
        relay(h, 0, 1, 5)
        moved[h, 1, 0].wait_recv()
        to_sib(h, far[h * 4], 1)
    far_chunk(0, 0)
    for h in range(2):
        relay(h, 1, 2, 5)
    far_chunk(1, 0)
    for h in range(2):
        for i, r in ((0, 3), (0, 2), (1, 1)):
            moved[h, i, r].wait_recv()
        to_sib(h, far[h * 4 + 1], 2)
    far_chunk(0, 1)
    for h in range(2):
        for i in range(2):
            moved[h, i, 4].wait_recv()
        to_sib(h, far[h * 4 + 2], 3)
    far_chunk(1, 1)
    far_chunk(0, 2)
    for h in range(2):
        for i in range(2):
            moved[h, i, 5].wait_recv()
        to_sib(h, far[h * 4 + 3], 4)
    far_chunk(1, 2)
    far_chunk(0, 3)
    far_chunk(1, 3)

    def distance(o):
        return (1 - o // 2) * (2 - o) + (o // 2) * (9 - 3 * o)

    def send(p, o, half):
        two = pl.ds(2 * half, 2)
        return rcopy(
            sb.at[p, o, two], rin.at[p, o, two], ss.at[p, o, half], sr.at[p, o, half], along(p, distance(o))
        )

    @pl.loop(0, 4)
    def _(o):
        d = distance(o)
        for half in range(2):
            for p in range(2):
                j = ((x, y)[p] + d) % 4
                for i in (2 * half, 2 * half + 1):
                    for u in range(2):
                        e = ((j * 4 + i) if p == 0 else (i * 4 + j)) * 4 + 2 * p + u
                        r, s = ex[0, e], ex[1, e]
                        left, right = [], []
                        for q in range(3):
                            for h in range(2):
                                a = xs[q, h, r]
                                left.append(
                                    jnp.concatenate(
                                        [a, jnp.concatenate([a[:, 128:], -a[:, :128]], axis=1)], axis=0
                                    )
                                )
                                right.append(xs[q, h, s])
                        v = lax.dot_general(
                            jnp.concatenate(left, axis=1),
                            jnp.concatenate(right, axis=1),
                            NT,
                            preferred_element_type=F32,
                        )
                        v = jnp.concatenate([v[:64], v[64:]], axis=1)
                        sb[p, o, i, u] = v.astype(BF16)
                        sf[p, i, u] = v

                @pl.when(o < 3)
                def _():
                    send(p, o, half).start()

    sent = []
    for p in range(2):
        total = sf[p]
        for o in range(3):
            for half in range(2):
                cp = send(p, o, half)
                sent.append(cp)
                cp.wait_recv()
            total = total + rin[p, o].astype(F32)
        af[p] = total
        ab[p] = total.astype(BF16)
        for d in range(1, 4):
            cp = rcopy(
                ab.at[p, (cell[p] + d) % 4], qin.at[p, d - 1], qs.at[p, d - 1], qr.at[p, d - 1], cross(p, d)
            )
            cp.start()
            sent.append(cp)
    for p in range(2):
        total = af[p, cell[p]]
        for d in range(1, 4):
            sent[p * 9 + 5 + d].wait_recv()
            total = total + qin[p, d - 1].astype(F32)
        cf[2 * p : 2 * p + 2] = total
        cb[2 * p : 2 * p + 2] = total.astype(BF16)
    wc = []
    for j in range(3):
        cp = rcopy(cb.at[(zl + j + 1) % 4], zin.at[j], ws.at[j], wr.at[j], wdev[j])
        cp.start()
        wc.append(cp)
    total = cf[zl]
    for j in range(3):
        wc[j].wait_recv()
        total = total + zin[j].astype(F32)
    out[...] = total * factor
    for cps in (moved, sibs):
        for cp in cps.values():
            cp.wait_send()
    for cp in pc + sent + wc:
        cp.wait_send()


def fused(factor, match, ex, lists, coeff, lin):
    smem = pl.BlockSpec(memory_space=pltpu.SMEM)
    vmem = pl.BlockSpec(memory_space=pltpu.VMEM)
    hbm = pl.BlockSpec(memory_space=pl.ANY)
    dma = pltpu.SemaphoreType.DMA

    def kern(*refs):
        fused_kernel(factor, *refs)

    scratch = [pltpu.VMEM((4, 4, 4, 2, 16, 128), BF16)] * 2 + [
        pltpu.VMEM((4, n, 4, 2, 16, 128), BF16) for n in (4, 4, 2, 2)
    ] * 2
    scratch += [
        pltpu.VMEM((145, 64, 128), BF16),
        pltpu.VMEM((3, 16, 1024, 128), BF16),
        pltpu.VMEM((3, 2, 1024, 256), F32),
        pltpu.VMEM((3, 2, 16, 64, 256), BF16),
        pltpu.VMEM((2, 4, 2, 64, 128), F32),
        pltpu.VMEM((2, 4, 4, 2, 64, 128), BF16),
        pltpu.VMEM((2, 3, 4, 2, 64, 128), BF16),
        pltpu.VMEM((2, 4, 2, 64, 128), F32),
        pltpu.VMEM((2, 4, 2, 64, 128), BF16),
        pltpu.VMEM((2, 3, 2, 64, 128), BF16),
        pltpu.VMEM((4, 64, 128), F32),
        pltpu.VMEM((4, 64, 128), BF16),
        pltpu.VMEM((3, 64, 128), BF16),
        pltpu.VMEM((3, 256), jnp.int32),
        pltpu.SMEM((4,), jnp.int32),
        pltpu.SMEM((3, 256), jnp.int32),
        dma((6,)),
    ]
    for shape in ((7, 2), (2, 3), (2, 2, 6), (2, 5), (2, 3, 2), (2, 3), (3,)):
        scratch += [dma(shape)] * 2
    return pl.pallas_call(
        kern,
        out_shape=jax.ShapeDtypeStruct((64, 128), F32),
        in_specs=[smem] * 2 + [vmem] + [hbm] * 2,
        out_specs=vmem,
        scratch_shapes=scratch,
        compiler_params=pltpu.CompilerParams(
            collective_id=0, has_side_effects=True, vmem_limit_bytes=60 * 2**20
        ),
        name="fused",
    )(match, ex, lists, coeff, lin)


def on_device(integrals, block_lists, coeff, match, ex_blocks):
    nq, naux, occ = 3, 64, 256
    factor = -((nq * naux * occ) ** (-0.5))
    lin = integrals.reshape(144, 64, 128)
    return fused(factor, match, ex_blocks[0], block_lists[:, 0, 0], coeff, lin)[None]


def solution(mesh):
    return jax.shard_map(
        on_device,
        mesh=mesh,
        in_specs=(
            P(None, "ka", "fit", None, None, None),
            P(None, "ka", "fit", None, None),
            P("ka", None, "fit", None),
            P(),
            P("ka", None, None),
        ),
        out_specs=P("ka", "fit", None),
        check_vma=False,
    )
```
